32 devices in a mesh: frames: 8 (over z, x), heads: 4 (over y, core).
Axes of the slice: x: 2, y: 2, z: 4, core: 2. Of those that a mesh axis runs over, the one named last changes fastest.
Arguments:
- queries: bfloat16 [1024, 4096], P('frames', 'heads'), may hold values from -9 to 9
- keys: bfloat16 [1024, 512], P(('frames', 'heads')), may hold values from -4.5 to 4.5
- values: bfloat16 [1024, 512], P(('frames', 'heads')), may hold values from -6 to 6
- block_mask: int32 [8, 8], replicated, may hold values from 0 to 1, as said below
- lengths: int32 [8], replicated, may hold values from 64 to 128, as said below
Outputs:
- attended: bfloat16 [1024, 4096], P('frames', 'heads')
The draws below stay inside these ranges and needn't reach their ends.
Inputs may be any that keep to these rules, and one draw needn't show every extreme that they name: block_mask[i, i] = 1 and block_mask[i, j] = 0 for j > i. `lengths`: some frame group is full in every draw.
All inputs are finite; a program needn't handle non-finite values.
Results may differ from the reference program's by a relative error of at most 0.0055.
Values may be sent and summed in bfloat16 or wider, within the bound.
A program may use at most 64 MiB of HBM per device.

```python
import jax
import jax.numpy as jnp
from jax import lax

HEAD_DIM = 128
Q_HEADS = 32
KV_HEADS = 4
TOK_DEV = 128
GROUPS = 8
TOKENS = 1024


def draw_keys(key, part):
    base = jnp.clip(jax.random.normal(jax.random.fold_in(key, 11), (TOKENS, KV_HEADS * HEAD_DIM), jnp.float32), -4.5, 4.5)
    return base.astype(jnp.bfloat16)


def draw_queries(key, part):
    base = jnp.clip(jax.random.normal(jax.random.fold_in(key, 13), (TOKENS, Q_HEADS * HEAD_DIM), jnp.float32), -4.5, 4.5)
    return base.astype(jnp.bfloat16)


def draw_block_mask(key, part):
    draws = jax.random.randint(jax.random.fold_in(key, 19), (GROUPS, GROUPS), 0, 5)
    rows = jnp.arange(GROUPS, dtype=jnp.int32)[:, None]
    cols = jnp.arange(GROUPS, dtype=jnp.int32)[None, :]
    below = (rows > cols) & (draws < 3)
    return jnp.where(below | (rows == cols), 1, 0).astype(jnp.int32)


def draw_lengths(key, part):
    counts = jax.random.randint(jax.random.fold_in(key, 23), (GROUPS,), TOK_DEV // 2, TOK_DEV + 1)
    chosen = jax.random.randint(jax.random.fold_in(key, 29), (), 0, GROUPS)
    return jnp.where(jnp.arange(GROUPS, dtype=jnp.int32) == chosen, TOK_DEV, counts).astype(jnp.int32)


def steps_of(rng, shape, cuts, least, top_value):
    gain, own = 1.0, jax.random.fold_in(rng, 6)
    for dim, blocks in cuts:
        steps = jnp.exp(jax.random.uniform(jax.random.fold_in(own, dim), (blocks,), jnp.float32, least / len(cuts), top_value / len(cuts)))
        gain = gain * jnp.repeat(steps, shape[dim] // blocks).reshape([-1 if axis == dim else 1 for axis in range(len(shape))])
    return gain


def noise(rng, extent, scale, limit, cuts=(), held_as=jnp.bfloat16):
    level = steps_of(rng, extent, cuts, -0.22, 0.18) if cuts else 1.0
    array = jax.random.normal(rng, extent, jnp.float32) * scale * level
    return jnp.minimum(jnp.maximum(array, -limit), limit).astype(held_as)


def setup_inputs(seed: int = 0) -> dict:
    arg_keys = jax.random.split(jax.random.key(seed), 6)
    queries = draw_queries(jax.random.fold_in(arg_keys[5], 71), 0)
    keys = draw_keys(jax.random.fold_in(arg_keys[5], 71), 0)
    values = noise(arg_keys[2], (TOKENS, KV_HEADS * HEAD_DIM), 1.0, 6.0, ((0, 32),))
    block_mask = draw_block_mask(jax.random.fold_in(arg_keys[5], 71), 0)
    lengths = draw_lengths(jax.random.fold_in(arg_keys[5], 71), 0)
    return dict(queries=queries, keys=keys, values=values, block_mask=block_mask, lengths=lengths)


masked_score = -1.0e30


def reference(queries, keys, values, block_mask, lengths):
    per_kv = Q_HEADS // KV_HEADS
    scale = HEAD_DIM ** -0.5
    key_rows = keys.astype(jnp.float32).reshape(TOKENS, KV_HEADS, HEAD_DIM)
    value_rows = values.astype(jnp.float32).reshape(TOKENS, KV_HEADS, HEAD_DIM)
    positions = jnp.arange(TOKENS, dtype=jnp.int32)
    key_group = positions // TOK_DEV
    within = positions % TOK_DEV
    key_live = within < lengths[key_group]
    grouped = queries.reshape(GROUPS, TOK_DEV, KV_HEADS, per_kv, HEAD_DIM)

    def one_group(index):
        query_rows = grouped[index].astype(jnp.float32)
        scores = jnp.einsum("tkgd,skd->kgts", query_rows, key_rows, precision=lax.Precision.HIGHEST) * scale
        valid = key_live & (block_mask[index][key_group] > 0)
        scores = jnp.where(valid[None, None, None, :], scores, masked_score)
        top = jnp.max(scores, axis=-1, keepdims=True)
        probs = jnp.exp(scores - top)
        total = jnp.sum(probs, axis=-1)
        rounded = probs.astype(jnp.bfloat16).astype(jnp.float32)
        summed = jnp.einsum("kgts,skd->tkgd", rounded, value_rows, precision=lax.Precision.HIGHEST)
        output = summed / jnp.transpose(total, (2, 0, 1))[..., None]
        return output.astype(jnp.bfloat16).reshape(TOK_DEV, Q_HEADS * HEAD_DIM)

    result = lax.map(one_group, jnp.arange(GROUPS, dtype=jnp.int32))
    return result.reshape(TOKENS, Q_HEADS * HEAD_DIM)
```

```python
import functools
import math

import jax
import jax.numpy as jnp
from jax import lax
from jax.experimental import pallas as pl
from jax.experimental.pallas import tpu as pltpu
from jax.sharding import PartitionSpec as P

HEAD_DIM = 128
MESH = pl.DeviceIdType.MESH
masked_score = -1e30


def kernel(
    frames,
    heads,
    lanes,
    mask_ref,
    len_ref,
    q_ref,
    k_ref,
    v_ref,
    out_ref,
    kv,
    qt,
    top,
    total,
    acc,
    send_sem,
    recv_sem,
    pass_send,
    pass_recv,
    own_sem,
):
    f = lax.axis_index("frames")
    h = lax.axis_index("heads")
    steps = frames // lanes
    hi = f // lanes
    lo = f % lanes
    piece = k_ref.shape[0]
    width = kv.shape[3]
    tokens = kv.shape[2]
    rows = q_ref.shape[0]
    q_local = q_ref.shape[1] // HEAD_DIM
    per_kv = q_local // (width // HEAD_DIM)
    mate = f + 1 - 2 * lo if lanes == 2 else f
    factor = HEAD_DIM**-0.5 * math.log2(math.e)

    barrier = pltpu.get_barrier_semaphore()

    def greet(d, carry):
        def one(r, inner):
            pl.semaphore_signal(
                barrier,
                inc=1,
                device_id=((hi - d) * lanes + lo, (h + r) % heads),
                device_id_type=MESH,
            )
            return inner

        return lax.fori_loop(jnp.where(d == 0, 1, 0), heads, one, carry)

    if lanes == 2:
        pl.semaphore_signal(barrier, inc=1, device_id=(mate, h), device_id_type=MESH)
    lax.fori_loop(0, hi + 1, greet, 0)
    pl.semaphore_wait(barrier, (steps - hi) * heads - 1 + (lanes - 1))

    def piece_copy(which, source, to_hi, to_h):
        target = to_hi * lanes + lo
        columns = pl.ds(pl.multiple_of(to_h * width, width), width)
        return pltpu.make_async_remote_copy(
            src_ref=source.at[:, columns],
            dst_ref=kv.at[f, which, pl.ds(pl.multiple_of(h * piece, piece), piece), :],
            send_sem=send_sem.at[to_hi - hi],
            recv_sem=recv_sem.at[hi],
            device_id=(target, to_h),
            device_id_type=MESH,
        )

    def send(i, carry):
        to_hi = steps - 1 - i
        start = jnp.where(to_hi == hi, 1, 0)

        def one(r, inner):
            to_h = (h + r) % heads
            piece_copy(0, k_ref, to_hi, to_h).start()
            piece_copy(1, v_ref, to_hi, to_h).start()
            return inner

        return lax.fori_loop(start, heads, one, carry)

    lax.fori_loop(0, steps - hi, send, 0)

    mine = pl.ds(pl.multiple_of(h * width, width), width)
    place = pl.ds(pl.multiple_of(h * piece, piece), piece)
    own = [
        pltpu.make_async_copy(source.at[:, mine], kv.at[f, which, place, :], own_sem.at[which])
        for which, source in ((0, k_ref), (1, v_ref))
    ]
    for copy in own:
        copy.start()

    for g in range(q_local):
        cols = slice(g * HEAD_DIM, (g + 1) * HEAD_DIM)
        qt[:, g * rows : (g + 1) * rows] = q_ref[:, cols].T
    top[...] = jnp.full_like(top, masked_score)
    total[...] = jnp.zeros_like(total)
    acc[...] = jnp.zeros_like(acc)
    for copy in own:
        copy.wait()

    def attend(group):
        limit = jnp.where(mask_ref[f, group] > 0, len_ref[group], 0)
        live = lax.broadcasted_iota(jnp.int32, (tokens, rows), 0) < limit
        for c in range(width // HEAD_DIM):
            cols = slice(c * HEAD_DIM, (c + 1) * HEAD_DIM)
            kb = kv[group, 0, :, cols]
            vt = kv[group, 1, :, cols].T
            for g in range(c * per_kv, (c + 1) * per_kv):
                at = slice(g * rows, (g + 1) * rows)
                s = jnp.dot(kb, qt[:, at], preferred_element_type=jnp.float32)
                s = jnp.where(live, s, masked_score)
                old = top[:, at]
                new = jnp.maximum(old, jnp.max(s, axis=0, keepdims=True))
                p = jnp.exp2((s - new) * factor)
                scale = jnp.exp2((old - new) * factor)
                top[:, at] = new
                total[:, at] = total[:, at] * scale + jnp.sum(p, axis=0, keepdims=True)
                acc[:, at] = acc[:, at] * scale + jnp.dot(
                    vt, p.astype(jnp.bfloat16), preferred_element_type=jnp.float32
                )

    def landed(group, sem):
        pltpu.make_async_copy(kv.at[group], kv.at[group], sem).wait()

    def pass_copy(group, slot):
        return pltpu.make_async_remote_copy(
            src_ref=kv.at[group],
            dst_ref=kv.at[group],
            send_sem=pass_send.at[slot],
            recv_sem=pass_recv.at[slot],
            device_id=(mate, h),
            device_id_type=MESH,
        )

    rest = kv.at[f, :, pl.ds(0, (heads - 1) * piece), :]
    pltpu.make_async_copy(rest, rest, recv_sem.at[hi]).wait()
    if lanes == 2:

        @pl.when(lo == 0)
        def _():
            pass_copy(f, hi).start()

    attend(f)

    def step(d, carry):
        from_hi = hi - d
        group = from_hi * lanes + lo
        landed(group, recv_sem.at[from_hi])
        if lanes == 2:
            pass_copy(group, from_hi).start()
        attend(group)
        if lanes == 2:
            other = from_hi * lanes + 1 - lo
            landed(other, pass_recv.at[from_hi])
            attend(other)
        return carry

    if lanes == 2:

        @pl.when(lo == 1)
        def _():
            landed(mate, pass_recv.at[hi])
            attend(mate)

    lax.fori_loop(1, hi + 1, step, 0)

    for g in range(q_local):
        at = slice(g * rows, (g + 1) * rows)
        done = (acc[:, at] / total[:, at]).T
        out_ref[:, g * HEAD_DIM : (g + 1) * HEAD_DIM] = done.astype(out_ref.dtype)

    pltpu.make_async_copy(rest, rest, send_sem.at[0]).wait()

    def drain(d, carry):
        pltpu.make_async_copy(kv.at[f], kv.at[f], send_sem.at[d]).wait()
        return carry

    lax.fori_loop(1, steps - hi, drain, 0)
    if lanes == 2:

        @pl.when(lo == 0)
        def _():
            pass_copy(f, hi).wait_send()

        def drain_pass(d, carry):
            pass_copy((hi - d) * lanes + lo, hi - d).wait_send()
            return carry

        lax.fori_loop(1, hi + 1, drain_pass, 0)


def solution(mesh):
    frames, heads = mesh.shape["frames"], mesh.shape["heads"]
    lanes = 2 if frames % 2 == 0 else 1

    def local(queries, keys, values, block_mask, lengths):
        rows, q_columns = queries.shape
        tokens = keys.shape[0] * heads
        width = keys.shape[1] // heads
        q_local = q_columns // HEAD_DIM
        steps = frames // lanes
        vmem = pl.BlockSpec(memory_space=pltpu.VMEM)
        smem = pl.BlockSpec(memory_space=pltpu.SMEM)
        return pl.pallas_call(
            functools.partial(kernel, frames, heads, lanes),
            out_shape=jax.ShapeDtypeStruct(queries.shape, queries.dtype),
            in_specs=[smem, smem, vmem, vmem, vmem],
            out_specs=vmem,
            scratch_shapes=[
                pltpu.VMEM((frames, 2, tokens, width), jnp.bfloat16),
                pltpu.VMEM((HEAD_DIM, q_local * rows), jnp.bfloat16),
                pltpu.VMEM((1, q_local * rows), jnp.float32),
                pltpu.VMEM((1, q_local * rows), jnp.float32),
                pltpu.VMEM((HEAD_DIM, q_local * rows), jnp.float32),
                pltpu.SemaphoreType.DMA((steps,)),
                pltpu.SemaphoreType.DMA((steps,)),
                pltpu.SemaphoreType.DMA((steps,)),
                pltpu.SemaphoreType.DMA((steps,)),
                pltpu.SemaphoreType.DMA((2,)),
            ],
            compiler_params=pltpu.CompilerParams(collective_id=0, has_side_effects=True),
        )(block_mask, lengths, queries, keys, values)

    return jax.shard_map(
        local,
        mesh=mesh,
        in_specs=(
            P("frames", "heads"),
            P(("frames", "heads"), None),
            P(("frames", "heads"), None),
            P(),
            P(),
        ),
        out_specs=P("frames", "heads"),
        check_vma=False,
    )
```

```python
import functools
import math

import jax
import jax.numpy as jnp
from jax import lax
from jax.experimental import pallas as pl
from jax.experimental.pallas import tpu as pltpu
from jax.sharding import PartitionSpec as P

HEAD_DIM = 128
MESH = pl.DeviceIdType.MESH
masked_score = -1e30


def kernel(
    frames,
    heads,
    lanes,
    mask_ref,
    len_ref,
    q_ref,
    k_ref,
    v_ref,
    out_ref,
    kv,
    q,
    qt,
    top,
    total,
    acc,
    mate_send,
    mate_recv,
    up_send,
    up_recv,
    side_send,
    side_recv,
    own_sem,
):
    f = lax.axis_index("frames")
    h = lax.axis_index("heads")
    steps = frames // lanes
    hi = f // lanes
    lo = f % lanes
    piece = k_ref.shape[0]
    width = kv.shape[3]
    tokens = kv.shape[2]
    rows = q_ref.shape[0]
    q_local = q_ref.shape[1] // HEAD_DIM
    per_kv = q_local // (width // HEAD_DIM)
    factor = HEAD_DIM**-0.5 * math.log2(math.e)
    partner = f + 1 - 2 * lo if lanes == 2 else f
    not_last = hi < steps - 1
    sends_side = (lo == 0) | (hi > 0)
    takes_side = (lo == 1) | (hi > 0)

    pair = 2 if heads % 2 == 0 else 1
    mates = [
        ((h // pair + j) % (heads // pair)) * pair + (h % pair + c) % pair
        for j in range(heads // pair)
        for c in range(pair)
    ][1:]

    barrier = pltpu.get_barrier_semaphore()

    def greet(device):
        pl.semaphore_signal(barrier, inc=1, device_id=device, device_id_type=MESH)

    @pl.when(hi > 0)
    def _():
        greet((f - lanes, h))

    for mate in mates:
        greet((f, mate))
    expected = heads - 1 + jnp.where(not_last, 1, 0)
    if lanes == 2:

        @pl.when(takes_side)
        def _():
            greet((partner, h))

        expected += jnp.where(sends_side, 1, 0)

    load_q = pltpu.make_async_copy(q_ref, q, own_sem.at[2])
    load_q.start()

    def rows_of(head):
        return pl.ds(pl.multiple_of(head * piece, piece), piece)

    mine = pl.ds(pl.multiple_of(h * width, width), width)
    sources = ((0, k_ref), (1, v_ref))
    own = [
        pltpu.make_async_copy(source.at[:, mine], kv.at[f, which, rows_of(h), :], own_sem.at[which])
        for which, source in sources
    ]
    for copy in own:
        copy.start()

    pl.semaphore_wait(barrier, expected)

    def remote(source, target, send, recv, device):
        return pltpu.make_async_remote_copy(
            src_ref=source,
            dst_ref=target,
            send_sem=send,
            recv_sem=recv,
            device_id=device,
            device_id_type=MESH,
        )

    for mate in mates[::-1]:
        columns = pl.ds(pl.multiple_of(mate * width, width), width)
        for which, source in sources:
            remote(
                source.at[:, columns],
                kv.at[f, which, rows_of(h), :],
                mate_send.at[0],
                mate_recv.at[h],
                (f, mate),
            ).start()

    def up(source, target, group_hi, head):
        remote(
            source, target, up_send.at[group_hi], up_recv.at[group_hi, head], (f + lanes, h)
        ).start()

    def side(source, target, group_hi):
        remote(
            source, target, side_send.at[group_hi], side_recv.at[group_hi], (partner, h)
        ).start()

    @pl.when(not_last)
    def _():
        for which, source in sources:
            up(source.at[:, mine], kv.at[f, which, rows_of(h), :], hi, h)

    if lanes == 2:

        @pl.when(lo == 0)
        def _():
            for which, source in sources:
                side(source.at[:, mine], kv.at[f, which, rows_of(h), :], hi)

    def landed(part, sem):
        pltpu.make_async_copy(part, part, sem).wait()

    def relay(group, group_hi, head, across):
        part = kv.at[group, :, rows_of(head), :]

        @pl.when(not_last)
        def _():
            up(part, part, group_hi, head)

        if lanes == 2:

            @pl.when(across)
            def _():
                side(part, part, group_hi)

    load_q.wait()
    for g in range(q_local):
        cols = slice(g * HEAD_DIM, (g + 1) * HEAD_DIM)
        qt[:, g * rows : (g + 1) * rows] = q[:, cols].T
    top[...] = jnp.full_like(top, masked_score)
    total[...] = jnp.zeros_like(total)
    acc[...] = jnp.zeros_like(acc)

    def attend(group):
        limit = jnp.where(mask_ref[f, group] > 0, len_ref[group], 0)
        live = lax.broadcasted_iota(jnp.int32, (tokens, rows), 0) < limit
        for c in range(width // HEAD_DIM):
            cols = slice(c * HEAD_DIM, (c + 1) * HEAD_DIM)
            kb = kv[group, 0, :, cols]
            vt = kv[group, 1, :, cols].T
            for g in range(c * per_kv, (c + 1) * per_kv):
                at = slice(g * rows, (g + 1) * rows)
                s = jnp.dot(kb, qt[:, at], preferred_element_type=jnp.float32)
                s = jnp.where(live, s, masked_score)
                old = top[:, at]
                new = jnp.maximum(old, jnp.max(s, axis=0, keepdims=True))
                p = jnp.exp2((s - new) * factor)
                scale = jnp.exp2((old - new) * factor)
                top[:, at] = new
                total[:, at] = total[:, at] * scale + jnp.sum(p, axis=0, keepdims=True)
                acc[:, at] = acc[:, at] * scale + jnp.dot(
                    vt, p.astype(jnp.bfloat16), preferred_element_type=jnp.float32
                )

    for mate in mates:
        landed(kv.at[f, :, rows_of(mate), :], mate_recv.at[mate])
        relay(f, hi, mate, lo == 0)
    for copy in own:
        copy.wait()
    attend(f)

    def attend_side(group_hi):
        group = group_hi * lanes + 1 - lo
        landed(kv.at[group], side_recv.at[group_hi])
        attend(group)

    def step(d, carry):
        group_hi = hi - d
        group = group_hi * lanes + lo
        for head in [h] + mates:
            landed(kv.at[group, :, rows_of(head), :], up_recv.at[group_hi, head])
            relay(group, group_hi, head, hi > 0)
        if lanes == 2:

            @pl.when((d > 1) | (lo == 1))
            def _():
                attend_side(group_hi + 1)

        attend(group)
        return carry

    lax.fori_loop(1, hi + 1, step, 0)
    if lanes == 2:

        @pl.when(takes_side)
        def _():
            attend_side(0)

    for g in range(q_local):
        at = slice(g * rows, (g + 1) * rows)
        done = (acc[:, at] / total[:, at]).T
        out_ref[:, g * HEAD_DIM : (g + 1) * HEAD_DIM] = done.astype(out_ref.dtype)

    rest = kv.at[f, :, pl.ds(0, (heads - 1) * piece), :]
    landed(rest, mate_send.at[0])

    @pl.when(not_last)
    def _():
        def drain(d, carry):
            landed(kv.at[f], up_send.at[hi - d])
            return carry

        lax.fori_loop(0, hi + 1, drain, 0)

    if lanes == 2:

        def drain_side(d, carry):
            landed(kv.at[f], side_send.at[hi - d])
            return carry

        lax.fori_loop(lo, hi + 1, drain_side, 0)


def solution(mesh):
    frames, heads = mesh.shape["frames"], mesh.shape["heads"]
    lanes = 2 if frames % 2 == 0 else 1

    def local(queries, keys, values, block_mask, lengths):
        rows, q_columns = queries.shape
        tokens = keys.shape[0] * heads
        width = keys.shape[1] // heads
        q_local = q_columns // HEAD_DIM
        steps = frames // lanes
        vmem = pl.BlockSpec(memory_space=pltpu.VMEM)
        hbm = pl.BlockSpec(memory_space=pl.ANY)
        smem = pl.BlockSpec(memory_space=pltpu.SMEM)
        return pl.pallas_call(
            functools.partial(kernel, frames, heads, lanes),
            out_shape=jax.ShapeDtypeStruct(queries.shape, queries.dtype),
            in_specs=[smem, smem, hbm, hbm, hbm],
            out_specs=vmem,
            scratch_shapes=[
                pltpu.VMEM((frames, 2, tokens, width), jnp.bfloat16),
                pltpu.VMEM(queries.shape, queries.dtype),
                pltpu.VMEM((HEAD_DIM, q_local * rows), jnp.bfloat16),
                pltpu.VMEM((1, q_local * rows), jnp.float32),
                pltpu.VMEM((1, q_local * rows), jnp.float32),
                pltpu.VMEM((HEAD_DIM, q_local * rows), jnp.float32),
                pltpu.SemaphoreType.DMA((1,)),
                pltpu.SemaphoreType.DMA((heads,)),
                pltpu.SemaphoreType.DMA((steps,)),
                pltpu.SemaphoreType.DMA((steps, heads)),
                pltpu.SemaphoreType.DMA((steps,)),
                pltpu.SemaphoreType.DMA((steps,)),
                pltpu.SemaphoreType.DMA((3,)),
            ],
            compiler_params=pltpu.CompilerParams(collective_id=0, has_side_effects=True),
        )(block_mask, lengths, queries, keys, values)

    return jax.shard_map(
        local,
        mesh=mesh,
        in_specs=(
            P("frames", "heads"),
            P(("frames", "heads"), None),
            P(("frames", "heads"), None),
            P(),
            P(),
        ),
        out_specs=P("frames", "heads"),
        check_vma=False,
    )
```

```python
import functools
import math

import jax
import jax.numpy as jnp
from jax import lax
from jax.experimental import pallas as pl
from jax.experimental.pallas import tpu as pltpu
from jax.sharding import PartitionSpec as P

HEAD_DIM = 128
MESH = pl.DeviceIdType.MESH
masked_score = -1e30


def kernel(
    frames,
    heads,
    lanes,
    mask_ref,
    len_ref,
    q_ref,
    k_ref,
    v_ref,
    out_ref,
    kv,
    q,
    qt,
    top,
    total,
    acc,
    mate_send,
    mate_recv,
    up_send,
    up_recv,
    side_send,
    side_recv,
    own_sem,
):
    f = lax.axis_index("frames")
    h = lax.axis_index("heads")
    steps = frames // lanes
    hi = f // lanes
    lo = f % lanes
    piece = k_ref.shape[0]
    width = kv.shape[3]
    tokens = kv.shape[2]
    rows = q_ref.shape[0]
    q_local = q_ref.shape[1] // HEAD_DIM
    per_kv = q_local // (width // HEAD_DIM)
    factor = HEAD_DIM**-0.5 * math.log2(math.e)
    partner = f + 1 - 2 * lo if lanes == 2 else f

    pair = 2 if heads % 2 == 0 else 1
    mates = [
        ((h // pair + j) % (heads // pair)) * pair + (h % pair + c) % pair
        for j in range(heads // pair)
        for c in range(pair)
    ][1:]

    barrier = pltpu.get_barrier_semaphore()

    def greet(device):
        pl.semaphore_signal(barrier, inc=1, device_id=device, device_id_type=MESH)

    def greet_down(from_hi, carry):
        greet((from_hi * lanes + lo, h))
        return carry

    lax.fori_loop(0, hi, greet_down, 0)
    for mate in mates[::-1]:
        greet((f, mate))
    expected = heads - 1 + steps - 1 - hi
    if lanes == 2:
        greet((partner, h))
        expected += 1

    load_q = pltpu.make_async_copy(q_ref, q, own_sem.at[2])
    load_q.start()

    def rows_of(head):
        return pl.ds(pl.multiple_of(head * piece, piece), piece)

    mine = pl.ds(pl.multiple_of(h * width, width), width)
    sources = ((0, k_ref), (1, v_ref))
    own = [
        pltpu.make_async_copy(source.at[:, mine], kv.at[f, which, rows_of(h), :], own_sem.at[which])
        for which, source in sources
    ]
    for copy in own:
        copy.start()

    pl.semaphore_wait(barrier, expected)

    def remote(source, target, send, recv, device):
        return pltpu.make_async_remote_copy(
            src_ref=source,
            dst_ref=target,
            send_sem=send,
            recv_sem=recv,
            device_id=device,
            device_id_type=MESH,
        )

    for mate in mates[::-1]:
        columns = pl.ds(pl.multiple_of(mate * width, width), width)
        for which, source in sources:
            remote(
                source.at[:, columns],
                kv.at[f, which, rows_of(h), :],
                mate_send.at[0],
                mate_recv.at[h],
                (f, mate),
            ).start()

    def up(source, target, to_hi, head):
        remote(
            source,
            target,
            up_send.at[to_hi],
            up_recv.at[hi, head],
            (to_hi * lanes + lo, h),
        ).start()

    def side(source, target, group_hi):
        remote(
            source, target, side_send.at[group_hi], side_recv.at[group_hi], (partner, h)
        ).start()

    if lanes == 2:

        @pl.when(lo == 0)
        def _():
            for which, source in sources:
                side(source.at[:, mine], kv.at[f, which, rows_of(h), :], hi)

    def landed(part, sem):
        pltpu.make_async_copy(part, part, sem).wait()

    def attend(group):
        limit = jnp.where(mask_ref[f, group] > 0, len_ref[group], 0)
        live = lax.broadcasted_iota(jnp.int32, (tokens, rows), 0) < limit
        for c in range(width // HEAD_DIM):
            cols = slice(c * HEAD_DIM, (c + 1) * HEAD_DIM)
            kb = kv[group, 0, :, cols]
            vt = kv[group, 1, :, cols].T
            for g in range(c * per_kv, (c + 1) * per_kv):
                at = slice(g * rows, (g + 1) * rows)
                s = jnp.dot(kb, qt[:, at], preferred_element_type=jnp.float32)
                s = jnp.where(live, s, masked_score)
                old = top[:, at]
                new = jnp.maximum(old, jnp.max(s, axis=0, keepdims=True))
                p = jnp.exp2((s - new) * factor)
                scale = jnp.exp2((old - new) * factor)
                top[:, at] = new
                total[:, at] = total[:, at] * scale + jnp.sum(p, axis=0, keepdims=True)
                acc[:, at] = acc[:, at] * scale + jnp.dot(
                    vt, p.astype(jnp.bfloat16), preferred_element_type=jnp.float32
                )

    far = steps - 1

    def up_all(head, parts):
        def one(d, carry):
            for source, target in parts:
                up(source, target, far - d, head)
            return carry

        lax.fori_loop(0, far - hi, one, 0)

    up_all(
        h, [(source.at[:, mine], kv.at[f, which, rows_of(h), :]) for which, source in sources]
    )
    load_q.wait()
    for g in range(q_local):
        cols = slice(g * HEAD_DIM, (g + 1) * HEAD_DIM)
        qt[:, g * rows : (g + 1) * rows] = q[:, cols].T
    top[...] = jnp.full_like(top, masked_score)
    total[...] = jnp.zeros_like(total)
    acc[...] = jnp.zeros_like(acc)
    for mate in mates:
        part = kv.at[f, :, rows_of(mate), :]
        landed(part, mate_recv.at[mate])
        up_all(mate, [(part, part)])
        if lanes == 2:

            @pl.when(lo == 0)
            def _():
                side(part, part, hi)

    for copy in own:
        copy.wait()

    def step(d, carry):
        group_hi = hi - d
        group = group_hi * lanes + lo

        @pl.when(d <= hi)
        def _():
            for head in [h] + mates:
                part = kv.at[group, :, rows_of(head), :]
                landed(part, up_recv.at[group_hi, head])
                if lanes == 2:
                    side(part, part, group_hi)

        attend(group + lanes)
        return carry

    lax.fori_loop(1, hi + 2, step, 0)

    if lanes == 2:

        def step_side(d, carry):
            group_hi = hi - d
            group = group_hi * lanes + 1 - lo
            landed(kv.at[group], side_recv.at[group_hi])
            attend(group)
            return carry

        lax.fori_loop(1 - lo, hi + 1, step_side, 0)

    for g in range(q_local):
        at = slice(g * rows, (g + 1) * rows)
        done = (acc[:, at] / total[:, at]).T
        out_ref[:, g * HEAD_DIM : (g + 1) * HEAD_DIM] = done.astype(out_ref.dtype)

    rest = kv.at[f, :, pl.ds(0, (heads - 1) * piece), :]
    landed(rest, mate_send.at[0])

    def drain(to_hi, carry):
        landed(kv.at[f], up_send.at[to_hi])
        return carry

    lax.fori_loop(hi + 1, steps, drain, 0)
    if lanes == 2:

        def drain_side(d, carry):
            landed(kv.at[f], side_send.at[hi - d])
            return carry

        lax.fori_loop(lo, hi + 1, drain_side, 0)


def solution(mesh):
    frames, heads = mesh.shape["frames"], mesh.shape["heads"]
    lanes = 2 if frames % 2 == 0 else 1

    def local(queries, keys, values, block_mask, lengths):
        rows, q_columns = queries.shape
        tokens = keys.shape[0] * heads
        width = keys.shape[1] // heads
        q_local = q_columns // HEAD_DIM
        steps = frames // lanes
        vmem = pl.BlockSpec(memory_space=pltpu.VMEM)
        hbm = pl.BlockSpec(memory_space=pl.ANY)
        smem = pl.BlockSpec(memory_space=pltpu.SMEM)
        return pl.pallas_call(
            functools.partial(kernel, frames, heads, lanes),
            out_shape=jax.ShapeDtypeStruct(queries.shape, queries.dtype),
            in_specs=[smem, smem, hbm, hbm, hbm],
            out_specs=vmem,
            scratch_shapes=[
                pltpu.VMEM((frames, 2, tokens, width), jnp.bfloat16),
                pltpu.VMEM(queries.shape, queries.dtype),
                pltpu.VMEM((HEAD_DIM, q_local * rows), jnp.bfloat16),
                pltpu.VMEM((1, q_local * rows), jnp.float32),
                pltpu.VMEM((1, q_local * rows), jnp.float32),
                pltpu.VMEM((HEAD_DIM, q_local * rows), jnp.float32),
                pltpu.SemaphoreType.DMA((1,)),
                pltpu.SemaphoreType.DMA((heads,)),
                pltpu.SemaphoreType.DMA((steps,)),
                pltpu.SemaphoreType.DMA((steps, heads)),
                pltpu.SemaphoreType.DMA((steps,)),
                pltpu.SemaphoreType.DMA((steps,)),
                pltpu.SemaphoreType.DMA((3,)),
            ],
            compiler_params=pltpu.CompilerParams(collective_id=0, has_side_effects=True),
        )(block_mask, lengths, queries, keys, values)

    return jax.shard_map(
        local,
        mesh=mesh,
        in_specs=(
            P("frames", "heads"),
            P(("frames", "heads"), None),
            P(("frames", "heads"), None),
            P(),
            P(),
        ),
        out_specs=P("frames", "heads"),
        check_vma=False,
    )
```

```python
import functools
import math

import jax
import jax.numpy as jnp
from jax import lax
from jax.experimental import pallas as pl
from jax.experimental.pallas import tpu as pltpu
from jax.sharding import PartitionSpec as P

HEAD_DIM = 128
MESH = pl.DeviceIdType.MESH
masked_score = -1e30


def kernel(
    frames,
    heads,
    lanes,
    mask_in,
    len_in,
    q_ref,
    k_ref,
    v_ref,
    out_ref,
    kv,
    q,
    qt,
    top,
    total,
    acc,
    mate_send,
    mate_recv,
    up_send,
    up_recv,
    side_send,
    side_recv,
    own_sem,
    mask_ref,
    len_ref,
):
    f = lax.axis_index("frames")
    h = lax.axis_index("heads")
    steps = frames // lanes
    hi = f // lanes
    lo = f % lanes
    piece = k_ref.shape[0]
    width = kv.shape[3]
    tokens = kv.shape[2]
    rows = q_ref.shape[0]
    q_local = q_ref.shape[1] // HEAD_DIM
    per_kv = q_local // (width // HEAD_DIM)
    factor = HEAD_DIM**-0.5 * math.log2(math.e)
    partner = f + 1 - 2 * lo if lanes == 2 else f

    pair = 2 if heads % 2 == 0 else 1
    mates = [
        ((h // pair + j) % (heads // pair)) * pair + (h % pair + c) % pair
        for j in range(heads // pair)
        for c in range(pair)
    ][1:]

    barrier = pltpu.get_barrier_semaphore()

    def greet(device):
        pl.semaphore_signal(barrier, inc=1, device_id=device, device_id_type=MESH)

    def greet_down(from_hi, carry):
        greet((from_hi * lanes + lo, h))
        return carry

    lax.fori_loop(0, hi, greet_down, 0)
    for mate in mates[::-1]:
        greet((f, mate))
    expected = heads - 1 + steps - 1 - hi
    if lanes == 2:
        greet((partner, h))
        expected += 1

    load_q = pltpu.make_async_copy(q_ref, q, own_sem.at[2])
    load_q.start()
    tables = [
        pltpu.make_async_copy(mask_in, mask_ref, own_sem.at[3]),
        pltpu.make_async_copy(len_in, len_ref, own_sem.at[4]),
    ]
    for copy in tables:
        copy.start()

    def rows_of(head):
        return pl.ds(pl.multiple_of(head * piece, piece), piece)

    mine = pl.ds(pl.multiple_of(h * width, width), width)
    sources = ((0, k_ref), (1, v_ref))
    own = [
        pltpu.make_async_copy(source.at[:, mine], kv.at[f, which, rows_of(h), :], own_sem.at[which])
        for which, source in sources
    ]
    for copy in own:
        copy.start()

    pl.semaphore_wait(barrier, expected)

    def remote(source, target, send, recv, device):
        return pltpu.make_async_remote_copy(
            src_ref=source,
            dst_ref=target,
            send_sem=send,
            recv_sem=recv,
            device_id=device,
            device_id_type=MESH,
        )

    for mate in mates[::-1]:
        columns = pl.ds(pl.multiple_of(mate * width, width), width)
        for which, source in sources:
            remote(
                source.at[:, columns],
                kv.at[f, which, rows_of(h), :],
                mate_send.at[0],
                mate_recv.at[h],
                (f, mate),
            ).start()

    def up(source, target, to_hi, head):
        remote(
            source,
            target,
            up_send.at[to_hi],
            up_recv.at[hi, head],
            (to_hi * lanes + lo, h),
        ).start()

    def side(source, target, group_hi):
        remote(
            source, target, side_send.at[group_hi], side_recv.at[group_hi], (partner, h)
        ).start()

    if lanes == 2:

        @pl.when(lo == 0)
        def _():
            for which, source in sources:
                side(source.at[:, mine], kv.at[f, which, rows_of(h), :], hi)

    def landed(part, sem):
        pltpu.make_async_copy(part, part, sem).wait()

    def attend(group):
        limit = jnp.where(mask_ref[f, group] > 0, len_ref[group], 0)
        live = lax.broadcasted_iota(jnp.int32, (tokens, rows), 0) < limit
        for c in range(width // HEAD_DIM):
            cols = slice(c * HEAD_DIM, (c + 1) * HEAD_DIM)
            kb = kv[group, 0, :, cols]
            vt = kv[group, 1, :, cols].T
            for g in range(c * per_kv, (c + 1) * per_kv):
                at = slice(g * rows, (g + 1) * rows)
                s = jnp.dot(kb, qt[:, at], preferred_element_type=jnp.float32)
                s = jnp.where(live, s, masked_score)
                old = top[:, at]
                new = jnp.maximum(old, jnp.max(s, axis=0, keepdims=True))
                p = jnp.exp2((s - new) * factor)
                scale = jnp.exp2((old - new) * factor)
                top[:, at] = new
                total[:, at] = total[:, at] * scale + jnp.sum(p, axis=0, keepdims=True)
                acc[:, at] = acc[:, at] * scale + jnp.dot(
                    vt, p.astype(jnp.bfloat16), preferred_element_type=jnp.float32
                )

    far = steps - 1

    def up_all(head, parts):
        def one(d, carry):
            for source, target in parts:
                up(source, target, far - d, head)
            return carry

        lax.fori_loop(0, far - hi, one, 0)

    up_all(
        h, [(source.at[:, mine], kv.at[f, which, rows_of(h), :]) for which, source in sources]
    )
    load_q.wait()
    for copy in tables:
        copy.wait()
    for g in range(q_local):
        cols = slice(g * HEAD_DIM, (g + 1) * HEAD_DIM)
        qt[:, g * rows : (g + 1) * rows] = q[:, cols].T
    top[...] = jnp.full_like(top, masked_score)
    total[...] = jnp.zeros_like(total)
    acc[...] = jnp.zeros_like(acc)
    for mate in mates:
        part = kv.at[f, :, rows_of(mate), :]
        landed(part, mate_recv.at[mate])
        up_all(mate, [(part, part)])
        if lanes == 2:

            @pl.when(lo == 0)
            def _():
                side(part, part, hi)

    for copy in own:
        copy.wait()

    def step(d, carry):
        group_hi = hi - d
        group = group_hi * lanes + lo

        @pl.when(d <= hi)
        def _():
            for head in [h] + mates:
                part = kv.at[group, :, rows_of(head), :]
                landed(part, up_recv.at[group_hi, head])
                if lanes == 2:
                    side(part, part, group_hi)

        attend(group + lanes)
        return carry

    lax.fori_loop(1, hi + 2, step, 0)

    if lanes == 2:

        def step_side(d, carry):
            group_hi = hi - d
            group = group_hi * lanes + 1 - lo
            landed(kv.at[group], side_recv.at[group_hi])
            attend(group)
            return carry

        lax.fori_loop(1 - lo, hi + 1, step_side, 0)

    for g in range(q_local):
        at = slice(g * rows, (g + 1) * rows)
        done = (acc[:, at] / total[:, at]).T
        out_ref[:, g * HEAD_DIM : (g + 1) * HEAD_DIM] = done.astype(out_ref.dtype)

    rest = kv.at[f, :, pl.ds(0, (heads - 1) * piece), :]
    landed(rest, mate_send.at[0])

    def drain(to_hi, carry):
        landed(kv.at[f], up_send.at[to_hi])
        return carry

    lax.fori_loop(hi + 1, steps, drain, 0)
    if lanes == 2:

        def drain_side(d, carry):
            landed(kv.at[f], side_send.at[hi - d])
            return carry

        lax.fori_loop(lo, hi + 1, drain_side, 0)


def solution(mesh):
    frames, heads = mesh.shape["frames"], mesh.shape["heads"]
    lanes = 2 if frames % 2 == 0 else 1

    def local(queries, keys, values, block_mask, lengths):
        rows, q_columns = queries.shape
        tokens = keys.shape[0] * heads
        width = keys.shape[1] // heads
        q_local = q_columns // HEAD_DIM
        steps = frames // lanes
        vmem = pl.BlockSpec(memory_space=pltpu.VMEM)
        hbm = pl.BlockSpec(memory_space=pltpu.HBM)
        pinned = [
            pltpu.with_memory_space_constraint(array, pltpu.HBM)
            for array in (block_mask, lengths, queries, keys, values)
        ]
        return pl.pallas_call(
            functools.partial(kernel, frames, heads, lanes),
            out_shape=jax.ShapeDtypeStruct(queries.shape, queries.dtype),
            in_specs=[hbm] * 5,
            out_specs=vmem,
            scratch_shapes=[
                pltpu.VMEM((frames, 2, tokens, width), jnp.bfloat16),
                pltpu.VMEM(queries.shape, queries.dtype),
                pltpu.VMEM((HEAD_DIM, q_local * rows), jnp.bfloat16),
                pltpu.VMEM((1, q_local * rows), jnp.float32),
                pltpu.VMEM((1, q_local * rows), jnp.float32),
                pltpu.VMEM((HEAD_DIM, q_local * rows), jnp.float32),
                pltpu.SemaphoreType.DMA((1,)),
                pltpu.SemaphoreType.DMA((heads,)),
                pltpu.SemaphoreType.DMA((steps,)),
                pltpu.SemaphoreType.DMA((steps, heads)),
                pltpu.SemaphoreType.DMA((steps,)),
                pltpu.SemaphoreType.DMA((steps,)),
                pltpu.SemaphoreType.DMA((5,)),
                pltpu.SMEM(block_mask.shape, jnp.int32),
                pltpu.SMEM(lengths.shape, jnp.int32),
            ],
            compiler_params=pltpu.CompilerParams(
                collective_id=0,
                has_side_effects=True,
                vmem_limit_bytes=frames * 4 * tokens * width + (8 << 20),
            ),
        )(*pinned)

    return jax.shard_map(
        local,
        mesh=mesh,
        in_specs=(
            P("frames", "heads"),
            P(("frames", "heads"), None),
            P(("frames", "heads"), None),
            P(),
            P(),
        ),
        out_specs=P("frames", "heads"),
        check_vma=False,
    )
```

```python
import functools
import math

import jax
import jax.numpy as jnp
from jax import lax
from jax.experimental import pallas as pl
from jax.experimental.pallas import tpu as pltpu
from jax.sharding import PartitionSpec as P

HEAD_DIM = 128
MESH = pl.DeviceIdType.MESH
masked_score = -1e30


def kernel(
    frames,
    heads,
    lanes,
    mask_in,
    len_in,
    q_ref,
    k_ref,
    v_ref,
    out_ref,
    kv,
    q,
    qt,
    top,
    total,
    acc,
    mate_send,
    mate_recv,
    up_send,
    up_recv,
    side_send,
    side_recv,
    own_sem,
    mask_ref,
    len_ref,
):
    f = lax.axis_index("frames")
    h = lax.axis_index("heads")
    steps = frames // lanes
    hi = f // lanes
    lo = f % lanes
    piece = k_ref.shape[0]
    width = kv.shape[3]
    tokens = kv.shape[2]
    rows = q_ref.shape[0]
    q_local = q_ref.shape[1] // HEAD_DIM
    per_kv = q_local // (width // HEAD_DIM)
    factor = HEAD_DIM**-0.5 * math.log2(math.e)
    partner = f + 1 - 2 * lo if lanes == 2 else f

    pair = 2 if heads % 2 == 0 else 1
    mates = [
        ((h // pair + j) % (heads // pair)) * pair + (h % pair + c) % pair
        for j in range(heads // pair)
        for c in range(pair)
    ][1:]

    barrier = pltpu.get_barrier_semaphore()

    def greet(device):
        pl.semaphore_signal(barrier, inc=1, device_id=device, device_id_type=MESH)

    def greet_down(from_hi, carry):
        greet((from_hi * lanes + lo, h))
        return carry

    lax.fori_loop(0, hi, greet_down, 0)
    for mate in mates[::-1]:
        greet((f, mate))
    expected = heads - 1 + steps - 1 - hi
    if lanes == 2:
        greet((partner, h))
        expected += 1

    load_q = pltpu.make_async_copy(q_ref, q, own_sem.at[2])
    load_q.start()
    tables = [
        pltpu.make_async_copy(mask_in, mask_ref, own_sem.at[3]),
        pltpu.make_async_copy(len_in, len_ref, own_sem.at[4]),
    ]
    for copy in tables:
        copy.start()

    def rows_of(head):
        return pl.ds(pl.multiple_of(head * piece, piece), piece)

    mine = pl.ds(pl.multiple_of(h * width, width), width)
    sources = ((0, k_ref), (1, v_ref))
    own = [
        pltpu.make_async_copy(source.at[:, mine], kv.at[f, which, rows_of(h), :], own_sem.at[which])
        for which, source in sources
    ]
    for copy in own:
        copy.start()

    pl.semaphore_wait(barrier, expected)

    def remote(source, target, send, recv, device):
        return pltpu.make_async_remote_copy(
            src_ref=source,
            dst_ref=target,
            send_sem=send,
            recv_sem=recv,
            device_id=device,
            device_id_type=MESH,
        )

    for mate in mates[::-1]:
        columns = pl.ds(pl.multiple_of(mate * width, width), width)
        for which, source in sources:
            remote(
                source.at[:, columns],
                kv.at[f, which, rows_of(h), :],
                mate_send.at[0],
                mate_recv.at[h],
                (f, mate),
            ).start()

    def up(source, target, to_hi, head):
        remote(
            source,
            target,
            up_send.at[to_hi],
            up_recv.at[hi, head // pair],
            (to_hi * lanes + lo, h),
        ).start()

    def side(source, target, group_hi):
        remote(
            source, target, side_send.at[group_hi], side_recv.at[group_hi], (partner, h)
        ).start()

    if lanes == 2:

        @pl.when(lo == 0)
        def _():
            for which, source in sources:
                side(source.at[:, mine], kv.at[f, which, rows_of(h), :], hi)

    def landed(part, sem):
        pltpu.make_async_copy(part, part, sem).wait()

    def attend(group):
        limit = jnp.where(mask_ref[f, group] > 0, len_ref[group], 0)
        live = lax.broadcasted_iota(jnp.int32, (tokens, rows), 0) < limit
        for c in range(width // HEAD_DIM):
            cols = slice(c * HEAD_DIM, (c + 1) * HEAD_DIM)
            kb = kv[group, 0, :, cols]
            vt = kv[group, 1, :, cols].T
            for g in range(c * per_kv, (c + 1) * per_kv):
                at = slice(g * rows, (g + 1) * rows)
                s = jnp.dot(kb, qt[:, at], preferred_element_type=jnp.float32)
                s = jnp.where(live, s, masked_score)
                old = top[:, at]
                new = jnp.maximum(old, jnp.max(s, axis=0, keepdims=True))
                p = jnp.exp2((s - new) * factor)
                scale = jnp.exp2((old - new) * factor)
                top[:, at] = new
                total[:, at] = total[:, at] * scale + jnp.sum(p, axis=0, keepdims=True)
                acc[:, at] = acc[:, at] * scale + jnp.dot(
                    vt, p.astype(jnp.bfloat16), preferred_element_type=jnp.float32
                )

    far = steps - 1

    def up_all(head, parts):
        def one(d, carry):
            for source, target in parts:
                up(source, target, far - d, head)
            return carry

        lax.fori_loop(0, far - hi, one, 0)

    up_all(
        h, [(source.at[:, mine], kv.at[f, which, rows_of(h), :]) for which, source in sources]
    )
    load_q.wait()
    for copy in tables:
        copy.wait()
    for g in range(q_local):
        cols = slice(g * HEAD_DIM, (g + 1) * HEAD_DIM)
        qt[:, g * rows : (g + 1) * rows] = q[:, cols].T
    top[...] = jnp.full_like(top, masked_score)
    total[...] = jnp.zeros_like(total)
    acc[...] = jnp.zeros_like(acc)
    for mate in mates:
        part = kv.at[f, :, rows_of(mate), :]
        landed(part, mate_recv.at[mate])
        up_all(mate, [(part, part)])
        if lanes == 2:

            @pl.when(lo == 0)
            def _():
                side(part, part, hi)

    for copy in own:
        copy.wait()

    def step(d, carry):
        group_hi = hi - d
        group = group_hi * lanes + lo

        @pl.when(d <= hi)
        def _():
            for head in ([h] + mates)[::pair]:
                both = head // pair
                span = pl.ds(pl.multiple_of(both * pair * piece, pair * piece), pair * piece)
                part = kv.at[group, :, span, :]
                landed(part, up_recv.at[group_hi, both])
                if lanes == 2:
                    side(part, part, group_hi)

        attend(group + lanes)
        return carry

    lax.fori_loop(1, hi + 2, step, 0)

    if lanes == 2:

        def step_side(d, carry):
            group_hi = hi - d
            group = group_hi * lanes + 1 - lo
            landed(kv.at[group], side_recv.at[group_hi])
            attend(group)
            return carry

        lax.fori_loop(1 - lo, hi + 1, step_side, 0)

    for g in range(q_local):
        at = slice(g * rows, (g + 1) * rows)
        done = (acc[:, at] / total[:, at]).T
        out_ref[:, g * HEAD_DIM : (g + 1) * HEAD_DIM] = done.astype(out_ref.dtype)

    rest = kv.at[f, :, pl.ds(0, (heads - 1) * piece), :]
    landed(rest, mate_send.at[0])

    def drain(to_hi, carry):
        landed(kv.at[f], up_send.at[to_hi])
        return carry

    lax.fori_loop(hi + 1, steps, drain, 0)
    if lanes == 2:

        def drain_side(d, carry):
            landed(kv.at[f], side_send.at[hi - d])
            return carry

        lax.fori_loop(lo, hi + 1, drain_side, 0)


def solution(mesh):
    frames, heads = mesh.shape["frames"], mesh.shape["heads"]
    lanes = 2 if frames % 2 == 0 else 1

    def local(queries, keys, values, block_mask, lengths):
        rows, q_columns = queries.shape
        tokens = keys.shape[0] * heads
        width = keys.shape[1] // heads
        q_local = q_columns // HEAD_DIM
        steps = frames // lanes
        vmem = pl.BlockSpec(memory_space=pltpu.VMEM)
        hbm = pl.BlockSpec(memory_space=pltpu.HBM)
        pinned = [
            pltpu.with_memory_space_constraint(array, pltpu.HBM)
            for array in (block_mask, lengths, queries, keys, values)
        ]
        return pl.pallas_call(
            functools.partial(kernel, frames, heads, lanes),
            out_shape=jax.ShapeDtypeStruct(queries.shape, queries.dtype),
            in_specs=[hbm] * 5,
            out_specs=vmem,
            scratch_shapes=[
                pltpu.VMEM((frames, 2, tokens, width), jnp.bfloat16),
                pltpu.VMEM(queries.shape, queries.dtype),
                pltpu.VMEM((HEAD_DIM, q_local * rows), jnp.bfloat16),
                pltpu.VMEM((1, q_local * rows), jnp.float32),
                pltpu.VMEM((1, q_local * rows), jnp.float32),
                pltpu.VMEM((HEAD_DIM, q_local * rows), jnp.float32),
                pltpu.SemaphoreType.DMA((1,)),
                pltpu.SemaphoreType.DMA((heads,)),
                pltpu.SemaphoreType.DMA((steps,)),
                pltpu.SemaphoreType.DMA((steps, heads // (2 if heads % 2 == 0 else 1))),
                pltpu.SemaphoreType.DMA((steps,)),
                pltpu.SemaphoreType.DMA((steps,)),
                pltpu.SemaphoreType.DMA((5,)),
                pltpu.SMEM(block_mask.shape, jnp.int32),
                pltpu.SMEM(lengths.shape, jnp.int32),
            ],
            compiler_params=pltpu.CompilerParams(
                collective_id=0,
                has_side_effects=True,
                vmem_limit_bytes=frames * 4 * tokens * width + (8 << 20),
            ),
        )(*pinned)

    return jax.shard_map(
        local,
        mesh=mesh,
        in_specs=(
            P("frames", "heads"),
            P(("frames", "heads"), None),
            P(("frames", "heads"), None),
            P(),
            P(),
        ),
        out_specs=P("frames", "heads"),
        check_vma=False,
    )
```
